256 devices in a mesh: row: 32 (over z, y), col: 8 (over x, core).
Axes of the slice: x: 4, y: 4, z: 8, core: 2. Of those that a mesh axis runs over, the one named last changes fastest.
Arguments:
- factor: float32 [32, 3, 1024, 4, 1024], P('row', None, None, None, 'col'), may hold values from -0.01953125 to 0.01953125
- knowns: float32 [32, 3, 1024, 256], P('row'), may hold values from -6 to 6
- inverse: float32 [4, 1024, 1024], P(None, None, 'col'), may hold values from -0.1875 to 0.1875
Outputs:
- solved: float32 [4, 1024, 256], P(None, 'col', 'row')
The draws below stay inside these ranges and needn't reach their ends.
All inputs are finite; a program needn't handle non-finite values.
Results may differ from the reference program's by a relative error of at most 0.0001.
Values sent between devices are 32-bit elements; how exact they have to be, the bound alone decides.
A program may use at most 64 MiB of HBM per device.

```python
import jax
import jax.numpy as jnp
from jax import lax

NB = 1024
NBLK = 96
SRC = 256
KW = 4
ROWGRID = 32
BPR = 3
ORDER = 98304


def level_of(key, shape, shards, least, largest):
    level = 1.0
    for axis_at, blocks in shards:
        draws = jax.random.uniform(jax.random.fold_in(jax.random.fold_in(key, 6), axis_at), (blocks,), jnp.float32, least / len(shards), largest / len(shards))
        level = level * jnp.repeat(jnp.exp(draws), shape[axis_at] // blocks).reshape((-1,) + (1,) * (len(shape) - 1 - axis_at))
    return level


def noise(rng, shape, spread, most, split=(), kind=jnp.bfloat16):
    entries = spread * jax.random.normal(rng, shape, jnp.float32)
    if split:
        entries = entries * level_of(rng, shape, split, -0.22, 0.18)
    return jnp.clip(entries, -most, most).astype(kind)


def setup_inputs(seed: int = 0) -> dict:
    splits = jax.random.split(jax.random.key(seed), 4)
    factor = noise(splits[0], (ROWGRID, BPR, NB, KW, NB), ORDER ** -0.5, 0.01953125, ((0, 32), (4, 8)), jnp.float32)
    knowns = noise(splits[1], (ROWGRID, BPR, NB, SRC), 1.0, 6.0, ((0, 32),), jnp.float32)
    inverse = noise(splits[2], (KW, NB, NB), NB ** -0.5, 0.1875, ((2, 8),), jnp.float32)
    return dict(factor=factor, knowns=knowns, inverse=inverse)


def reference(factor, knowns, inverse):
    first_block = NBLK - KW
    blockid = jnp.arange(BPR, dtype=jnp.int32)[None, :] * ROWGRID + jnp.arange(ROWGRID, dtype=jnp.int32)[:, None]
    keep_mask = (blockid < first_block).astype(knowns.dtype)
    masked = knowns * keep_mask[:, :, None, None]

    def add_rows(running, pieces):
        piece_factor, piece_knowns = pieces
        return running + jnp.einsum("lajc,las->jcs", piece_factor, piece_knowns, precision=lax.Precision.HIGHEST), None

    prefix, _ = lax.scan(add_rows, jnp.zeros((KW, NB, SRC), knowns.dtype), (factor, masked))
    solved = []
    for step in range(KW):
        block_id = first_block + step
        residual = knowns[block_id % ROWGRID, block_id // ROWGRID] - prefix[step]
        for earlier in range(step):
            other = first_block + earlier
            rows_block = factor[other % ROWGRID, other // ROWGRID, :, step, :]
            residual = residual - jnp.dot(rows_block.T, solved[earlier], precision=lax.Precision.HIGHEST)
        solved.append(jnp.dot(inverse[step].T, residual, precision=lax.Precision.HIGHEST))
    return jnp.stack(solved)
```

```python
import jax
import jax.numpy as jnp
from jax import lax
from jax.experimental import pallas as pl
from jax.experimental.pallas import tpu as pltpu
from jax.sharding import PartitionSpec as P

MESH = pl.DeviceIdType.MESH
KW = 4
NY = 4
LANE = 128
STEP = 512
PARTS = 4
F32 = jnp.float32
BF16 = jnp.bfloat16
POINTS = (3, 5, 8, 12)
HOP = 2


def halves(value):
    high = value.astype(BF16)
    low = (value - high.astype(F32)).astype(BF16)
    return high, low


def mul(a, b):
    return jnp.dot(a, b, preferred_element_type=F32)


def kernel(
    sizes,
    fac, kn, inv, out,
    fbuf, kbuf, dbuf, kth, ktl, acc, ybuf, zsrc, zbuf, tfull, racc, cbuf, lhs,
    dh, dl, ubuf, uh, ul, xfull, csrc, obuf,
    fsem, ksem, dsem, ysend, yrecv, zsend, zrecv, tsend, trecv, xsend, xrecv,
    csend, crecv, usend, urecv, osend, orecv,
):
    nz, nc, nl, nb, ns = sizes
    sp = ns // nz
    so = sp // NY
    per = nb // STEP
    row, col = lax.axis_index("row"), lax.axis_index("col")
    z, y = lax.div(row, NY), lax.rem(row, NY)
    last = nz - 1
    nblk = NY - 1 - y
    nf = nblk * PARTS
    ends = (NY - 1) * PARTS + HOP * (nz - 1)
    crows = nb // (2 * PARTS)

    def remote(src, dst, ssem, rsem, to_row, to_col):
        return pltpu.make_async_remote_copy(
            src_ref=src, dst_ref=dst, send_sem=ssem, recv_sem=rsem,
            device_id=(to_row, to_col), device_id_type=MESH,
        )

    def load_f(c):
        rows = pl.ds(c * STEP * KW, STEP * KW)
        return pltpu.make_async_copy(fac.at[rows], fbuf.at[rows], fsem.at[c])

    def load_k(c):
        rows = pl.ds(c * STEP, STEP)
        return pltpu.make_async_copy(kn.at[rows], kbuf.at[rows], ksem.at[c])

    def load_d():
        return pltpu.make_async_copy(inv.at[y], dbuf, dsem)

    steps = nl * per
    own = (nl - 1) * per

    @pl.when(z == last)
    def _():
        for c in range(own, steps):
            load_f(c).start()

    for c in range(own):
        load_f(c).start()
        load_k(c).start()

    @pl.when(z < last)
    def _():
        for c in range(own, steps):
            load_f(c).start()

    for c in range(own, steps):
        load_k(c).start()
    load_d().start()

    barrier = pltpu.get_barrier_semaphore()
    for dy in range(NY):
        for dk in range(nc):
            if dy or dk:
                pl.semaphore_signal(
                    barrier, inc=1,
                    device_id=(z * NY + lax.rem(y + dy, NY), lax.rem(col + dk, nc)),
                    device_id_type=MESH,
                )
    for d in range(1, nz):
        pl.semaphore_signal(
            barrier, inc=1, device_id=(lax.rem(z + d, nz) * NY + y, col), device_id_type=MESH
        )
    pl.semaphore_wait(barrier, NY * nc - 1 + nz - 1)

    def piece(way, f):
        first = way * (nb // 2) + lax.rem(f, PARTS) * crows
        return ubuf.at[lax.div(f, PARTS), pl.ds(pl.multiple_of(first, 8), crows)]

    def pass_on(way, f):
        to = lax.rem(z + (1 if way == 0 else nz - 1), nz)
        part = piece(way, f)
        return remote(part, part, usend.at[way, f], urecv.at[way, f], to * NY + y, col)

    @pl.when(z == last)
    def _():
        for c in range(own, steps):
            load_f(c).wait()

        @pl.loop(0, nf)
        def _(f):
            j = y + 1 + lax.div(f, PARTS)
            for way in (0, 1):
                first = way * (nb // 2) + lax.rem(f, PARTS) * crows
                start = (nl - 1) * nb * KW + first * KW + j
                ubuf[lax.div(f, PARTS), pl.ds(pl.multiple_of(first, 8), crows), :] = fbuf[
                    pl.ds(start, crows, stride=KW), :
                ]
                pass_on(way, f).start()

    def at_end(way):
        return (z == last - 1) if way == 0 else (z == 0)

    def relay(since, until):
        @pl.when(z < last)
        def _():
            @pl.loop(since, until)
            def _(t):
                for way in (0, 1):
                    hop = z + 1 if way == 0 else last - z
                    f = t - HOP * hop

                    @pl.when(jnp.logical_and(f >= 0, f < nf))
                    def _():
                        pass_on(way, f).wait_recv()

                        @pl.when(jnp.logical_not(at_end(way)))
                        def _():
                            pass_on(way, f).start()

    def multiply(c, half, first):
        rows = pl.ds(pl.multiple_of(c * STEP, STEP), STEP)
        if half == 0:
            load_f(c).wait()
            load_k(c).wait()
            high, low = halves(kbuf[rows, :].T)
            kth[c] = high
            ktl[c] = low
        else:
            high, low = kth[c], ktl[c]
        fh, fl = [], []
        for j in (2 * half, 2 * half + 1):
            a, b = halves(fbuf[pl.ds(c * STEP * KW + j, STEP, stride=KW), :])
            fh.append(a)
            fl.append(b)
        fh, fl = jnp.concatenate(fh, axis=1), jnp.concatenate(fl, axis=1)
        got = mul(high, fh) + mul(low, fh) + mul(high, fl)
        for n in (0, 1):
            part = got[:, n * LANE:(n + 1) * LANE]
            if first:
                acc[2 * half + n] = part
            else:
                acc[2 * half + n] += part

    def to_row(j):
        slot = lax.rem(y - j + NY, NY) - 1
        return remote(acc.at[j], ybuf.at[slot], ysend.at[j], yrecv.at[slot], z * NY + j, col)

    for half in (0, 1):
        multiply(0, half, True)

        @pl.loop(1, own)
        def _(c):
            multiply(c, half, False)

        @pl.when(z < last)
        def _():
            @pl.loop(own, steps)
            def _(c):
                multiply(c, half, False)

        for j in (2 * half, 2 * half + 1):
            @pl.when(y != j)
            def _():
                to_row(j).start()

        relay(0 if half == 0 else POINTS[half - 1], POINTS[half])

    load_d().wait()
    for c in range(per):
        rows = pl.ds(c * STEP, STEP)
        a, b = halves(dbuf[rows, :])
        dh[rows, :] = a
        dl[rows, :] = b

    @pl.when(z == last)
    def _():
        for c in range(own, steps):
            load_k(c).wait()
        first = pl.multiple_of((nl - 1) * nb + col * LANE, LANE)
        acc[y] -= kbuf[pl.ds(first, LANE), :].T

    for slot in range(NY - 1):
        remote(acc.at[0], ybuf.at[slot], ysend.at[0], yrecv.at[slot], row, col).wait_recv()
    zsrc[...] = acc[y] + ybuf[0] + ybuf[1] + ybuf[2]

    def to_plane(d):
        to = lax.rem(z + d, nz)
        return remote(
            zsrc.at[pl.ds(pl.multiple_of(to * sp, 8), sp)], zbuf.at[d - 1],
            zsend.at[d - 1], zrecv.at[d - 1], to * NY + y, col,
        )

    for d in range(1, nz):
        to_plane(d).start()
    relay(POINTS[1], POINTS[2])
    total = zsrc[pl.ds(pl.multiple_of(z * sp, 8), sp), :]
    for d in range(1, nz):
        to_plane(d).wait_recv()
        total += zbuf[d - 1]
    tfull[col] = total

    def to_cols(full, ssem, rsem, d):
        return remote(full.at[col], full.at[col], ssem.at[d - 1], rsem.at[d - 1], row, lax.rem(col + d, nc))

    def from_cols(full, ssem, rsem, d):
        slot = lax.rem(col - d + nc, nc)
        return remote(full.at[slot], full.at[slot], ssem.at[d - 1], rsem.at[d - 1], row, col)

    for d in range(1, nc):
        to_cols(tfull, tsend, trecv, d).start()
    relay(POINTS[2], POINTS[3])
    for d in range(1, nc):
        from_cols(tfull, tsend, trecv, d).wait_recv()
    racc[...] = -tfull[...]

    def split_u():
        @pl.loop(0, nblk)
        def _(b):
            for c in range(per):
                rows = pl.ds(c * STEP, STEP)
                a, l = halves(ubuf[b, rows, :])
                uh[b, rows, :] = a
                ul[b, rows, :] = l

    @pl.when(y > 0)
    def _():
        relay(POINTS[3], ends)
        split_u()

    @pl.loop(0, y)
    def _(i):
        for k in range(nc):
            remote(csrc.at[0], cbuf.at[i, k], csend.at[0, k], crecv.at[i, k], row, col).wait_recv()
        racc[...] -= cbuf[i]

    def fill(full):
        for k in range(nc):
            a, b = halves(full[k])
            lhs[0:sp, k * LANE:(k + 1) * LANE] = a
            lhs[sp:2 * sp, k * LANE:(k + 1) * LANE] = b

    def apply(high, low):
        both = mul(lhs[...], high)
        return both[0:sp] + both[sp:2 * sp] + mul(lhs[0:sp, :], low)

    fill(racc)
    xfull[col] = apply(dh[...], dl[...])

    @pl.when(y < NY - 1)
    def _():
        for d in range(1, nc):
            to_cols(xfull, xsend, xrecv, d).start()

    def to_owner(d):
        to = lax.rem(y + d, NY)
        return remote(
            xfull.at[col, pl.ds(pl.multiple_of(to * so, 8), so)], obuf.at[y],
            osend.at[d - 1], orecv.at[d - 1], z * NY + to, col,
        )

    for d in range(1, NY):
        to_owner(d).start()
    obuf[y] = xfull[col, pl.ds(pl.multiple_of(y * so, 8), so), :]

    @pl.when(y == 0)
    def _():
        relay(POINTS[3], ends)
        split_u()

    def to_later(b, k):
        return remote(
            csrc.at[b], cbuf.at[y, col], csend.at[b, k], crecv.at[y, col], z * NY + y + 1 + b, k
        )

    @pl.when(y < NY - 1)
    def _():
        for d in range(1, nc):
            from_cols(xfull, xsend, xrecv, d).wait_recv()
        fill(xfull)

        @pl.loop(0, nblk)
        def _(b):
            csrc[b] = apply(uh[b], ul[b])
            for k in range(nc):
                to_later(b, k).start()

    for d in range(1, NY):
        slot = lax.rem(y - d + NY, NY)
        remote(obuf.at[slot], obuf.at[slot], osend.at[d - 1], orecv.at[d - 1], row, col).wait_recv()
    out[...] = obuf[...]

    for j in range(NY):
        @pl.when(y != j)
        def _():
            to_row(j).wait_send()
    for d in range(1, nz):
        to_plane(d).wait_send()
    for d in range(1, nc):
        to_cols(tfull, tsend, trecv, d).wait_send()

    @pl.when(y < NY - 1)
    def _():
        for d in range(1, nc):
            to_cols(xfull, xsend, xrecv, d).wait_send()

        @pl.loop(0, nblk)
        def _(b):
            for k in range(nc):
                to_later(b, k).wait_send()

    for d in range(1, NY):
        to_owner(d).wait_send()

    @pl.loop(0, nf)
    def _(f):
        for way in (0, 1):
            @pl.when(jnp.logical_not(at_end(way)))
            def _():
                pass_on(way, f).wait_send()


def on_device(nz, nc, factor, knowns, inverse):
    _, nl, nb, _, lanes = factor.shape
    ns = knowns.shape[3]
    sp = ns // nz
    steps = nl * (nb // STEP)
    V, DMA = pltpu.VMEM, pltpu.SemaphoreType.DMA
    scratch = [
        V((nl * nb * KW, LANE), F32), V((nl * nb, ns), F32), V((nb, LANE), F32),
        V((steps, ns, STEP), BF16), V((steps, ns, STEP), BF16),
        V((KW, ns, LANE), F32), V((NY - 1, ns, LANE), F32),
        V((ns, LANE), F32), V((nz - 1, sp, LANE), F32),
        V((nc, sp, LANE), F32), V((nc, sp, LANE), F32),
        V((NY - 1, nc, sp, LANE), F32), V((2 * sp, nb), BF16),
        V((nb, LANE), BF16), V((nb, LANE), BF16),
        V((NY - 1, nb, LANE), F32), V((NY - 1, nb, LANE), BF16), V((NY - 1, nb, LANE), BF16),
        V((nc, sp, LANE), F32), V((NY - 1, sp, LANE), F32), V((KW, sp // NY, LANE), F32),
        DMA((steps,)), DMA((steps,)), DMA(()), DMA((NY,)), DMA((NY - 1,)),
        DMA((nz - 1,)), DMA((nz - 1,)), DMA((nc - 1,)), DMA((nc - 1,)), DMA((nc - 1,)), DMA((nc - 1,)),
        DMA((NY - 1, nc)), DMA((NY - 1, nc)),
        DMA((2, (NY - 1) * PARTS)), DMA((2, (NY - 1) * PARTS)), DMA((NY - 1,)), DMA((NY - 1,)),
    ]
    hbm = pl.BlockSpec(memory_space=pl.ANY)

    def body(*refs):
        kernel((nz, nc, nl, nb, ns), *refs)

    got = pl.pallas_call(
        body,
        out_shape=jax.ShapeDtypeStruct((KW, sp // NY, LANE), F32),
        in_specs=[hbm, hbm, hbm],
        out_specs=pl.BlockSpec(memory_space=pltpu.VMEM),
        scratch_shapes=scratch,
        compiler_params=pltpu.CompilerParams(
            collective_id=0, has_side_effects=True, vmem_limit_bytes=56 * 2 ** 20
        ),
        name="solve_window",
    )(
        factor.reshape(nl * nb * KW, lanes),
        knowns.reshape(nl * nb, ns),
        inverse,
    )
    return jnp.transpose(got, (0, 2, 1))


def solution(mesh):
    nz, nc = mesh.shape["row"] // NY, mesh.shape["col"]

    def step(factor, knowns, inverse):
        return on_device(nz, nc, factor, knowns, inverse)

    return jax.shard_map(
        step,
        mesh=mesh,
        in_specs=(
            P("row", None, None, None, "col"),
            P("row", None, None, None),
            P(None, None, "col"),
        ),
        out_specs=P(None, "col", "row"),
        check_vma=False,
    )
```

```python
import jax
import jax.numpy as jnp
from jax import lax
from jax.experimental import pallas as pl
from jax.experimental.pallas import tpu as pltpu
from jax.sharding import PartitionSpec as P

MESH = pl.DeviceIdType.MESH
KW = 4
NY = 4
LANE = 128
STEP = 512
TILE = 256
PARTS = 8
F32 = jnp.float32
BF16 = jnp.bfloat16
POINTS = (2, 10, 22, 30)
HOP = 4


def halves(value):
    high = value.astype(BF16)
    low = (value - high.astype(F32)).astype(BF16)
    return high, low


def mul(a, b):
    return jnp.dot(a, b, preferred_element_type=F32)


def kernel(
    sizes,
    fac, kn, inv, out,
    fbuf, kbuf, dfull, kth, ktl, acc, ybuf, zsrc, zbuf, tfull, racc, cbuf, lhs,
    dh, dl, ubuf, uh, ul, wh, wl, xfull, csrc, obuf,
    fsem, ksem, dsem, ysend, yrecv, zsend, zrecv, tsend, trecv, xsend, xrecv,
    csend, crecv, usend, urecv, osend, orecv, dsend, drecv,
):
    nz, nc, nl, nb, ns = sizes
    sp = ns // nz
    so = sp // NY
    per = nb // STEP
    row, col = lax.axis_index("row"), lax.axis_index("col")
    z, y = lax.div(row, NY), lax.rem(row, NY)
    last = nz - 1
    nblk = NY - 1 - y
    nf = nblk * PARTS
    crows = nb // (2 * PARTS)

    def remote(src, dst, ssem, rsem, to_row, to_col):
        return pltpu.make_async_remote_copy(
            src_ref=src, dst_ref=dst, send_sem=ssem, recv_sem=rsem,
            device_id=(to_row, to_col), device_id_type=MESH,
        )

    def load_f(c):
        rows = pl.ds(c * STEP * KW, STEP * KW)
        return pltpu.make_async_copy(fac.at[rows], fbuf.at[rows], fsem.at[c])

    def load_k(c):
        rows = pl.ds(c * STEP, STEP)
        return pltpu.make_async_copy(kn.at[rows], kbuf.at[rows], ksem.at[c])

    def load_d():
        return pltpu.make_async_copy(inv.at[y], dfull.at[col], dsem)

    steps = nl * per
    own = (nl - 1) * per

    load_d().start()

    @pl.when(z == last)
    def _():
        for c in range(own, steps):
            load_f(c).start()

    for c in range(own):
        load_f(c).start()
        load_k(c).start()

    @pl.when(z < last)
    def _():
        for c in range(own, steps):
            load_f(c).start()

    for c in range(own, steps):
        load_k(c).start()

    barrier = pltpu.get_barrier_semaphore()
    for dy in range(NY):
        for dk in range(nc):
            if dy or dk:
                pl.semaphore_signal(
                    barrier, inc=1,
                    device_id=(z * NY + lax.rem(y + dy, NY), lax.rem(col + dk, nc)),
                    device_id_type=MESH,
                )
    for d in range(1, nz):
        pl.semaphore_signal(
            barrier, inc=1, device_id=(lax.rem(z + d, nz) * NY + y, col), device_id_type=MESH
        )

    def piece(way, f):
        first = way * (nb // 2) + lax.rem(f, PARTS) * crows
        return ubuf.at[lax.div(f, PARTS), pl.ds(pl.multiple_of(first, 8), crows)]

    def pass_on(way, f):
        to = lax.rem(z + (1 if way == 0 else nz - 1), nz)
        part = piece(way, f)
        return remote(part, part, usend.at[way, f], urecv.at[way, f], to * NY + y, col)

    def feed():
        @pl.when(z == last)
        def _():
            for c in range(own, steps):
                load_f(c).wait()

            @pl.loop(0, nf)
            def _(f):
                j = y + 1 + lax.div(f, PARTS)
                for way in (0, 1):
                    first = way * (nb // 2) + lax.rem(f, PARTS) * crows
                    start = (nl - 1) * nb * KW + first * KW + j
                    ubuf[lax.div(f, PARTS), pl.ds(pl.multiple_of(first, 8), crows), :] = fbuf[
                        pl.ds(start, crows, stride=KW), :
                    ]
                    pass_on(way, f).start()

    core = lax.rem(col, 2)
    partner = col + 1 - 2 * core
    middle = jnp.logical_and(y > 0, y < NY - 1)

    def d_slot(d):
        return lax.rem(col + 2 * d, nc)

    def d_out(d):
        mine = dfull.at[col]
        return remote(mine, mine, dsend.at[d], drecv.at[col], row, d_slot(d) if d else partner)

    def d_relay(d):
        part = dfull.at[d_slot(d)]
        return remote(part, part, dsend.at[nc // 2 - 1 + d], drecv.at[d_slot(d)], row, partner)

    def d_in(slot):
        part = dfull.at[slot]
        return remote(part, part, dsend.at[0], drecv.at[slot], row, partner)

    def share_d():
        load_d().wait()

        @pl.when(middle)
        def _():
            for d in range(nc // 2):
                d_out(d).start()

    def take_d():
        for d in range(1, nc // 2):
            d_in(d_slot(d)).wait_recv()
            d_relay(d).start()
        for d in range(nc // 2):
            d_in(lax.rem(partner + 2 * d, nc)).wait_recv()

    def fold(count):
        high = jnp.concatenate([uh[b] for b in range(count)], axis=1)
        low = jnp.concatenate([ul[b] for b in range(count)], axis=1)

        @pl.loop(0, nb // TILE)
        def _(c):
            rows = pl.ds(pl.multiple_of(c * TILE, TILE), TILE)
            a, l = halves(jnp.concatenate([dfull[k, rows, :] for k in range(nc)], axis=1))
            got = mul(a, high) + mul(l, high) + mul(a, low)
            for b in range(count):
                wh[b, rows, :], wl[b, rows, :] = halves(got[:, b * LANE:(b + 1) * LANE])

    def at_end(way):
        return (z == last - 1) if way == 0 else (z == 0)

    def relay(since, until):
        @pl.when(z < last)
        def _():
            @pl.loop(since, until)
            def _(t):
                for way in (0, 1):
                    hop = z + 1 if way == 0 else last - z
                    f = t - HOP * hop

                    @pl.when(jnp.logical_and(f >= 0, f < nf))
                    def _():
                        pass_on(way, f).wait_recv()

                        @pl.when(jnp.logical_not(at_end(way)))
                        def _():
                            pass_on(way, f).start()

    def multiply(c, half, first):
        rows = pl.ds(pl.multiple_of(c * STEP, STEP), STEP)
        if half == 0:
            load_f(c).wait()
            load_k(c).wait()
            high, low = halves(kbuf[rows, :].T)
            kth[c] = high
            ktl[c] = low
        else:
            high, low = kth[c], ktl[c]
        fh, fl = [], []
        for j in (2 * half, 2 * half + 1):
            a, b = halves(fbuf[pl.ds(c * STEP * KW + j, STEP, stride=KW), :])
            fh.append(a)
            fl.append(b)
        fh, fl = jnp.concatenate(fh, axis=1), jnp.concatenate(fl, axis=1)
        got = mul(high, fh) + mul(low, fh) + mul(high, fl)
        for n in (0, 1):
            part = got[:, n * LANE:(n + 1) * LANE]
            if first:
                acc[2 * half + n] = part
            else:
                acc[2 * half + n] += part

    def to_row(j):
        slot = lax.rem(y - j + NY, NY) - 1
        return remote(acc.at[j], ybuf.at[slot], ysend.at[j], yrecv.at[slot], z * NY + j, col)

    for half in (0, 1):
        multiply(0, half, True)
        if half == 0:
            pl.semaphore_wait(barrier, NY * nc - 1 + nz - 1)
            feed()
            share_d()

        @pl.loop(1, own)
        def _(c):
            multiply(c, half, False)

        @pl.when(z < last)
        def _():
            @pl.loop(own, steps)
            def _(c):
                multiply(c, half, False)

        for j in (2 * half, 2 * half + 1):
            @pl.when(y != j)
            def _():
                to_row(j).start()

        relay(0 if half == 0 else POINTS[half - 1], POINTS[half])

    for c in range(per):
        rows = pl.ds(c * STEP, STEP)
        a, b = halves(dfull[col, rows, :])
        dh[rows, :] = a
        dl[rows, :] = b

    @pl.when(z == last)
    def _():
        for c in range(own, steps):
            load_k(c).wait()
        first = pl.multiple_of((nl - 1) * nb + col * LANE, LANE)
        acc[y] -= kbuf[pl.ds(first, LANE), :].T

    for slot in range(NY - 1):
        remote(acc.at[0], ybuf.at[slot], ysend.at[0], yrecv.at[slot], row, col).wait_recv()
    zsrc[...] = acc[y] + ybuf[0] + ybuf[1] + ybuf[2]

    def to_plane(d):
        to = lax.rem(z + d, nz)
        return remote(
            zsrc.at[pl.ds(pl.multiple_of(to * sp, 8), sp)], zbuf.at[d - 1],
            zsend.at[d - 1], zrecv.at[d - 1], to * NY + y, col,
        )

    for d in range(1, nz):
        to_plane(d).start()
    relay(POINTS[1], POINTS[2])
    total = zsrc[pl.ds(pl.multiple_of(z * sp, 8), sp), :]
    for d in range(1, nz):
        to_plane(d).wait_recv()
        total += zbuf[d - 1]
    tfull[col] = total

    def to_cols(full, ssem, rsem, d):
        return remote(full.at[col], full.at[col], ssem.at[d - 1], rsem.at[d - 1], row, lax.rem(col + d, nc))

    def from_cols(full, ssem, rsem, d):
        slot = lax.rem(col - d + nc, nc)
        return remote(full.at[slot], full.at[slot], ssem.at[d - 1], rsem.at[d - 1], row, col)

    for d in range(1, nc):
        to_cols(tfull, tsend, trecv, d).start()
    relay(POINTS[2], POINTS[3])
    for d in range(1, nc):
        from_cols(tfull, tsend, trecv, d).wait_recv()
    racc[...] = tfull[...]

    def split_u(b):
        for c in range(per):
            rows = pl.ds(c * STEP, STEP)
            a, l = halves(ubuf[b, rows, :])
            uh[b, rows, :] = a
            ul[b, rows, :] = l

    def finish(b):
        so_far = POINTS[3] if b == 0 else max(POINTS[3], PARTS * b + HOP * (nz - 1))
        relay(so_far, PARTS * (b + 1) + HOP * (nz - 1))
        split_u(b)

    for b in range(NY - 2):
        @pl.when(jnp.logical_and(y > 0, b < nblk))
        def _():
            finish(b)

    for count in range(1, NY - 1):
        @pl.when(y == NY - 1 - count)
        def _():
            take_d()
            fold(count)

    @pl.loop(0, y)
    def _(i):
        for k in range(nc):
            remote(csrc.at[0], cbuf.at[i, k], csend.at[0, k], crecv.at[i, k], row, col).wait_recv()
        racc[...] -= cbuf[i]

    def fill(full):
        for k in range(nc):
            a, b = halves(full[k])
            lhs[0:sp, k * LANE:(k + 1) * LANE] = a
            lhs[sp:2 * sp, k * LANE:(k + 1) * LANE] = b

    def apply(high, low):
        both = mul(lhs[...], high)
        return both[0:sp] + both[sp:2 * sp] + mul(lhs[0:sp, :], low)

    def to_later(b, k):
        return remote(
            csrc.at[b], cbuf.at[y, col], csend.at[b, k], crecv.at[y, col], z * NY + y + 1 + b, k
        )

    def correct(b, high, low):
        csrc[b] = apply(high[b], low[b])
        for k in range(nc):
            to_later(b, k).start()

    fill(racc)
    for count in range(1, NY - 1):
        @pl.when(y == NY - 1 - count)
        def _():
            for b in range(count):
                correct(b, wh, wl)

    xfull[col] = apply(dh[...], dl[...])

    @pl.when(y == 0)
    def _():
        for d in range(1, nc):
            to_cols(xfull, xsend, xrecv, d).start()

    def to_owner(d):
        to = lax.rem(y + d, NY)
        return remote(
            xfull.at[col, pl.ds(pl.multiple_of(to * so, 8), so)], obuf.at[y],
            osend.at[d - 1], orecv.at[d - 1], z * NY + to, col,
        )

    for d in range(1, NY):
        to_owner(d).start()
    obuf[y] = xfull[col, pl.ds(pl.multiple_of(y * so, 8), so), :]

    @pl.when(y == 0)
    def _():
        finish(0)
        for d in range(1, nc):
            from_cols(xfull, xsend, xrecv, d).wait_recv()
        fill(xfull)
        for b in range(NY - 1):
            if b > 0:
                finish(b)
            correct(b, uh, ul)

    for d in range(1, NY):
        slot = lax.rem(y - d + NY, NY)
        remote(obuf.at[slot], obuf.at[slot], osend.at[d - 1], orecv.at[d - 1], row, col).wait_recv()
    out[...] = obuf[...]

    for j in range(NY):
        @pl.when(y != j)
        def _():
            to_row(j).wait_send()
    for d in range(1, nz):
        to_plane(d).wait_send()
    for d in range(1, nc):
        to_cols(tfull, tsend, trecv, d).wait_send()

    @pl.when(y == 0)
    def _():
        for d in range(1, nc):
            to_cols(xfull, xsend, xrecv, d).wait_send()

    @pl.loop(0, nblk)
    def _(b):
        for k in range(nc):
            to_later(b, k).wait_send()

    @pl.when(middle)
    def _():
        for d in range(nc // 2):
            d_out(d).wait_send()
        for d in range(1, nc // 2):
            d_relay(d).wait_send()

    for d in range(1, NY):
        to_owner(d).wait_send()

    @pl.loop(0, nf)
    def _(f):
        for way in (0, 1):
            @pl.when(jnp.logical_not(at_end(way)))
            def _():
                pass_on(way, f).wait_send()


def on_device(nz, nc, factor, knowns, inverse):
    _, nl, nb, _, lanes = factor.shape
    ns = knowns.shape[3]
    sp = ns // nz
    steps = nl * (nb // STEP)
    V, DMA = pltpu.VMEM, pltpu.SemaphoreType.DMA
    scratch = [
        V((nl * nb * KW, LANE), F32), V((nl * nb, ns), F32), V((nc, nb, LANE), F32),
        V((steps, ns, STEP), BF16), V((steps, ns, STEP), BF16),
        V((KW, ns, LANE), F32), V((NY - 1, ns, LANE), F32),
        V((ns, LANE), F32), V((nz - 1, sp, LANE), F32),
        V((nc, sp, LANE), F32), V((nc, sp, LANE), F32),
        V((NY - 1, nc, sp, LANE), F32), V((2 * sp, nb), BF16),
        V((nb, LANE), BF16), V((nb, LANE), BF16),
        V((NY - 1, nb, LANE), F32), V((NY - 1, nb, LANE), BF16), V((NY - 1, nb, LANE), BF16),
        V((NY - 2, nb, LANE), BF16), V((NY - 2, nb, LANE), BF16),
        V((nc, sp, LANE), F32), V((NY - 1, sp, LANE), F32), V((KW, sp // NY, LANE), F32),
        DMA((steps,)), DMA((steps,)), DMA(()), DMA((NY,)), DMA((NY - 1,)),
        DMA((nz - 1,)), DMA((nz - 1,)), DMA((nc - 1,)), DMA((nc - 1,)), DMA((nc - 1,)), DMA((nc - 1,)),
        DMA((NY - 1, nc)), DMA((NY - 1, nc)),
        DMA((2, (NY - 1) * PARTS)), DMA((2, (NY - 1) * PARTS)), DMA((NY - 1,)), DMA((NY - 1,)),
        DMA((nc - 1,)), DMA((nc,)),
    ]
    hbm = pl.BlockSpec(memory_space=pl.ANY)

    def body(*refs):
        kernel((nz, nc, nl, nb, ns), *refs)

    got = pl.pallas_call(
        body,
        out_shape=jax.ShapeDtypeStruct((KW, sp // NY, LANE), F32),
        in_specs=[hbm, hbm, hbm],
        out_specs=pl.BlockSpec(memory_space=pltpu.VMEM),
        scratch_shapes=scratch,
        compiler_params=pltpu.CompilerParams(
            collective_id=0, has_side_effects=True, vmem_limit_bytes=56 * 2 ** 20
        ),
        name="solve_window",
    )(
        factor.reshape(nl * nb * KW, lanes),
        knowns.reshape(nl * nb, ns),
        inverse,
    )
    return -jnp.transpose(got, (0, 2, 1))


def solution(mesh):
    nz, nc = mesh.shape["row"] // NY, mesh.shape["col"]

    def step(factor, knowns, inverse):
        return on_device(nz, nc, factor, knowns, inverse)

    return jax.shard_map(
        step,
        mesh=mesh,
        in_specs=(
            P("row", None, None, None, "col"),
            P("row", None, None, None),
            P(None, None, "col"),
        ),
        out_specs=P(None, "col", "row"),
        check_vma=False,
    )
```

```python
import jax
import jax.numpy as jnp
from jax import lax
from jax.experimental import pallas as pl
from jax.experimental.pallas import tpu as pltpu
from jax.sharding import PartitionSpec as P

MESH = pl.DeviceIdType.MESH
KW = 4
NY = 4
LANE = 128
STEP = 512
TILE = 256
PARTS = 8
F32 = jnp.float32
BF16 = jnp.bfloat16
POINTS = (6, 15, 26, 33)
HOP = 4


def halves(value):
    high = value.astype(BF16)
    low = (value - high.astype(F32)).astype(BF16)
    return high, low


def mul(a, b):
    return jnp.dot(a, b, preferred_element_type=F32)


def kernel(
    sizes,
    fac, kn, inv, out,
    fbuf, kbuf, dfull, kth, ktl, acc, ybuf, zsrc, zbuf, tfull, racc, cbuf, lhs,
    dh, dl, ubuf, uh, ul, wh, wl, xfull, csrc, obuf,
    fsem, ksem, dsem, ysend, yrecv, zsend, zrecv, tsend, trecv, xsend, xrecv,
    csend, crecv, usend, urecv, osend, orecv, dsend, drecv,
):
    nz, nc, nl, nb, ns = sizes
    sp = ns // nz
    so = sp // NY
    per = nb // STEP
    row, col = lax.axis_index("row"), lax.axis_index("col")
    z, y = lax.div(row, NY), lax.rem(row, NY)
    last = nz - 1
    nblk = NY - 1 - y
    nf = nblk * PARTS
    crows = nb // (2 * PARTS)

    def remote(src, dst, ssem, rsem, to_row, to_col):
        return pltpu.make_async_remote_copy(
            src_ref=src, dst_ref=dst, send_sem=ssem, recv_sem=rsem,
            device_id=(to_row, to_col), device_id_type=MESH,
        )

    def load_f(c):
        rows = pl.ds(c * STEP * KW, STEP * KW)
        return pltpu.make_async_copy(fac.at[rows], fbuf.at[rows], fsem.at[c])

    def load_k(c):
        rows = pl.ds(c * STEP, STEP)
        return pltpu.make_async_copy(kn.at[rows], kbuf.at[rows], ksem.at[c])

    def load_d():
        return pltpu.make_async_copy(inv.at[y], dfull.at[col], dsem)

    steps = nl * per
    own = (nl - 1) * per

    load_d().start()

    @pl.when(z == last)
    def _():
        for c in range(own, steps):
            load_f(c).start()

    for c in range(own):
        load_f(c).start()
        load_k(c).start()

    @pl.when(z < last)
    def _():
        for c in range(own, steps):
            load_f(c).start()

    for c in range(own, steps):
        load_k(c).start()

    barrier = pltpu.get_barrier_semaphore()
    for dy in range(NY):
        for dk in range(nc):
            if dy or dk:
                pl.semaphore_signal(
                    barrier, inc=1,
                    device_id=(z * NY + lax.rem(y + dy, NY), lax.rem(col + dk, nc)),
                    device_id_type=MESH,
                )
    for d in range(1, nz):
        pl.semaphore_signal(
            barrier, inc=1, device_id=(lax.rem(z + d, nz) * NY + y, col), device_id_type=MESH
        )

    def enter():
        pl.semaphore_wait(barrier, NY * nc - 1 + nz - 1)

    def piece(way, f):
        first = way * (nb // 2) + lax.rem(f, PARTS) * crows
        return ubuf.at[lax.div(f, PARTS), pl.ds(pl.multiple_of(first, 8), crows)]

    def pass_on(way, f):
        to = lax.rem(z + (1 if way == 0 else nz - 1), nz)
        part = piece(way, f)
        return remote(part, part, usend.at[way, f], urecv.at[way, f], to * NY + y, col)

    def feed():
        for c in range(own, steps):
            load_f(c).wait()

        @pl.loop(0, nf)
        def _(f):
            j = y + 1 + lax.div(f, PARTS)
            for way in (0, 1):
                first = way * (nb // 2) + lax.rem(f, PARTS) * crows
                start = (nl - 1) * nb * KW + first * KW + j
                ubuf[lax.div(f, PARTS), pl.ds(pl.multiple_of(first, 8), crows), :] = fbuf[
                    pl.ds(start, crows, stride=KW), :
                ]
                pass_on(way, f).start()

    core = lax.rem(col, 2)
    partner = col + 1 - 2 * core
    middle = jnp.logical_and(y > 0, y < NY - 1)

    def d_slot(d):
        return lax.rem(col + 2 * d, nc)

    def d_out(d):
        mine = dfull.at[col]
        return remote(mine, mine, dsend.at[d], drecv.at[col], row, d_slot(d) if d else partner)

    def d_relay(d):
        part = dfull.at[d_slot(d)]
        return remote(part, part, dsend.at[nc // 2 - 1 + d], drecv.at[d_slot(d)], row, partner)

    def d_in(slot):
        part = dfull.at[slot]
        return remote(part, part, dsend.at[0], drecv.at[slot], row, partner)

    def share_d():
        load_d().wait()

        @pl.when(middle)
        def _():
            for d in range(nc // 2):
                d_out(d).start()

    def take_d():
        for d in range(1, nc // 2):
            d_in(d_slot(d)).wait_recv()
            d_relay(d).start()
        for d in range(nc // 2):
            d_in(lax.rem(partner + 2 * d, nc)).wait_recv()

    def fold(count):
        high, low = uh[count], ul[count]

        @pl.loop(0, nb // TILE)
        def _(c):
            rows = pl.ds(pl.multiple_of(c * TILE, TILE), TILE)
            a, l = halves(jnp.concatenate([dfull[k, rows, :] for k in range(nc)], axis=1))
            got = mul(a, high) + mul(l, high) + mul(a, low)
            wh[count, rows, :], wl[count, rows, :] = halves(got)

    def at_end(way):
        return (z == last - 1) if way == 0 else (z == 0)

    def relay(since, until):
        @pl.when(z < last)
        def _():
            @pl.loop(since, until)
            def _(t):
                for way in (0, 1):
                    hop = z + 1 if way == 0 else last - z
                    f = t - HOP * hop

                    @pl.when(jnp.logical_and(f >= 0, f < nf))
                    def _():
                        pass_on(way, f).wait_recv()

                        @pl.when(jnp.logical_not(at_end(way)))
                        def _():
                            pass_on(way, f).start()

    def multiply(c, half, first):
        rows = pl.ds(pl.multiple_of(c * STEP, STEP), STEP)
        if half == 0:
            load_f(c).wait()
            load_k(c).wait()
            high, low = halves(kbuf[rows, :].T)
            kth[c] = high
            ktl[c] = low
        else:
            high, low = kth[c], ktl[c]
        fh, fl = [], []
        for j in (2 * half, 2 * half + 1):
            a, b = halves(fbuf[pl.ds(c * STEP * KW + j, STEP, stride=KW), :])
            fh.append(a)
            fl.append(b)
        fh, fl = jnp.concatenate(fh, axis=1), jnp.concatenate(fl, axis=1)
        got = mul(high, fh) + mul(low, fh) + mul(high, fl)
        for n in (0, 1):
            part = got[:, n * LANE:(n + 1) * LANE]
            if first:
                acc[2 * half + n] = part
            else:
                acc[2 * half + n] += part

    def to_row(j):
        slot = lax.rem(y - j + NY, NY) - 1
        return remote(acc.at[j], ybuf.at[slot], ysend.at[j], yrecv.at[slot], z * NY + j, col)

    for half in (0, 1):
        if half == 0:
            @pl.when(z == last)
            def _():
                enter()
                feed()

        multiply(0, half, True)
        if half == 0:
            @pl.when(z < last)
            def _():
                enter()

            share_d()

        @pl.loop(1, own)
        def _(c):
            multiply(c, half, False)
            if half == 1:
                relay(POINTS[0] + c - 1, POINTS[0] + c)

        @pl.when(z < last)
        def _():
            @pl.loop(own, steps)
            def _(c):
                multiply(c, half, False)
                if half == 1:
                    relay(POINTS[0] + c - 1, POINTS[0] + c)

        for j in (2 * half, 2 * half + 1):
            @pl.when(y != j)
            def _():
                to_row(j).start()

        relay(0 if half == 0 else POINTS[0] + steps - 1, POINTS[half])

    for c in range(per):
        rows = pl.ds(c * STEP, STEP)
        a, b = halves(dfull[col, rows, :])
        dh[rows, :] = a
        dl[rows, :] = b

    @pl.when(z == last)
    def _():
        for c in range(own, steps):
            load_k(c).wait()
        first = pl.multiple_of((nl - 1) * nb + col * LANE, LANE)
        acc[y] -= kbuf[pl.ds(first, LANE), :].T

    for slot in range(NY - 1):
        remote(acc.at[0], ybuf.at[slot], ysend.at[0], yrecv.at[slot], row, col).wait_recv()
    zsrc[...] = acc[y] + ybuf[0] + ybuf[1] + ybuf[2]

    def to_plane(d):
        to = lax.rem(z + d, nz)
        return remote(
            zsrc.at[pl.ds(pl.multiple_of(to * sp, 8), sp)], zbuf.at[d - 1],
            zsend.at[d - 1], zrecv.at[d - 1], to * NY + y, col,
        )

    for d in range(1, nz):
        to_plane(d).start()
    relay(POINTS[1], POINTS[2])
    total = zsrc[pl.ds(pl.multiple_of(z * sp, 8), sp), :]
    for d in range(1, nz):
        to_plane(d).wait_recv()
        total += zbuf[d - 1]
    tfull[col] = total

    def to_cols(full, ssem, rsem, d):
        return remote(full.at[col], full.at[col], ssem.at[d - 1], rsem.at[d - 1], row, lax.rem(col + d, nc))

    def from_cols(full, ssem, rsem, d):
        slot = lax.rem(col - d + nc, nc)
        return remote(full.at[slot], full.at[slot], ssem.at[d - 1], rsem.at[d - 1], row, col)

    for d in range(1, nc):
        to_cols(tfull, tsend, trecv, d).start()
    relay(POINTS[2], POINTS[3])
    for d in range(1, nc):
        from_cols(tfull, tsend, trecv, d).wait_recv()
    racc[...] = tfull[...]

    def split_u(b):
        for c in range(per):
            rows = pl.ds(c * STEP, STEP)
            a, l = halves(ubuf[b, rows, :])
            uh[b, rows, :] = a
            ul[b, rows, :] = l

    def finish(b):
        so_far = POINTS[3] if b == 0 else max(POINTS[3], PARTS * b + HOP * (nz - 1))
        relay(so_far, PARTS * (b + 1) + HOP * (nz - 1))
        split_u(b)

    @pl.when(middle)
    def _():
        finish(0)
        take_d()
        fold(0)

    for b in range(1, NY - 2):
        @pl.when(jnp.logical_and(y > 0, b < nblk))
        def _():
            finish(b)

    @pl.loop(0, y)
    def _(i):
        for k in range(nc):
            remote(csrc.at[0], cbuf.at[i, k], csend.at[0, k], crecv.at[i, k], row, col).wait_recv()
        racc[...] -= cbuf[i]

    def fill(full):
        for k in range(nc):
            a, b = halves(full[k])
            lhs[0:sp, k * LANE:(k + 1) * LANE] = a
            lhs[sp:2 * sp, k * LANE:(k + 1) * LANE] = b

    def apply(high, low):
        both = mul(lhs[...], high)
        return both[0:sp] + both[sp:2 * sp] + mul(lhs[0:sp, :], low)

    def to_later(b, k):
        return remote(
            csrc.at[b], cbuf.at[y, col], csend.at[b, k], crecv.at[y, col], z * NY + y + 1 + b, k
        )

    def correct(b, high, low):
        csrc[b] = apply(high[b], low[b])
        for k in range(nc):
            to_later(b, k).start()

    fill(racc)
    for count in range(1, NY - 1):
        @pl.when(y == NY - 1 - count)
        def _():
            for b in range(count):
                if b:
                    fold(b)
                correct(b, wh, wl)

    xfull[col] = apply(dh[...], dl[...])

    @pl.when(y == 0)
    def _():
        for d in range(1, nc):
            to_cols(xfull, xsend, xrecv, d).start()

    def to_owner(d):
        to = lax.rem(y + d, NY)
        return remote(
            xfull.at[col, pl.ds(pl.multiple_of(to * so, 8), so)], obuf.at[y],
            osend.at[d - 1], orecv.at[d - 1], z * NY + to, col,
        )

    for d in range(1, NY):
        to_owner(d).start()
    obuf[y] = xfull[col, pl.ds(pl.multiple_of(y * so, 8), so), :]

    @pl.when(y == 0)
    def _():
        finish(0)
        for d in range(1, nc):
            from_cols(xfull, xsend, xrecv, d).wait_recv()
        fill(xfull)
        for b in range(NY - 1):
            if b > 0:
                finish(b)
            correct(b, uh, ul)

    for d in range(1, NY):
        slot = lax.rem(y - d + NY, NY)
        remote(obuf.at[slot], obuf.at[slot], osend.at[d - 1], orecv.at[d - 1], row, col).wait_recv()
    out[...] = obuf[...]

    for j in range(NY):
        @pl.when(y != j)
        def _():
            to_row(j).wait_send()
    for d in range(1, nz):
        to_plane(d).wait_send()
    for d in range(1, nc):
        to_cols(tfull, tsend, trecv, d).wait_send()

    @pl.when(y == 0)
    def _():
        for d in range(1, nc):
            to_cols(xfull, xsend, xrecv, d).wait_send()

    @pl.loop(0, nblk)
    def _(b):
        for k in range(nc):
            to_later(b, k).wait_send()

    @pl.when(middle)
    def _():
        for d in range(nc // 2):
            d_out(d).wait_send()
        for d in range(1, nc // 2):
            d_relay(d).wait_send()

    for d in range(1, NY):
        to_owner(d).wait_send()

    @pl.loop(0, nf)
    def _(f):
        for way in (0, 1):
            @pl.when(jnp.logical_not(at_end(way)))
            def _():
                pass_on(way, f).wait_send()


def on_device(nz, nc, factor, knowns, inverse):
    _, nl, nb, _, lanes = factor.shape
    ns = knowns.shape[3]
    sp = ns // nz
    steps = nl * (nb // STEP)
    V, DMA = pltpu.VMEM, pltpu.SemaphoreType.DMA
    scratch = [
        V((nl * nb * KW, LANE), F32), V((nl * nb, ns), F32), V((nc, nb, LANE), F32),
        V((steps, ns, STEP), BF16), V((steps, ns, STEP), BF16),
        V((KW, ns, LANE), F32), V((NY - 1, ns, LANE), F32),
        V((ns, LANE), F32), V((nz - 1, sp, LANE), F32),
        V((nc, sp, LANE), F32), V((nc, sp, LANE), F32),
        V((NY - 1, nc, sp, LANE), F32), V((2 * sp, nb), BF16),
        V((nb, LANE), BF16), V((nb, LANE), BF16),
        V((NY - 1, nb, LANE), F32), V((NY - 1, nb, LANE), BF16), V((NY - 1, nb, LANE), BF16),
        V((NY - 2, nb, LANE), BF16), V((NY - 2, nb, LANE), BF16),
        V((nc, sp, LANE), F32), V((NY - 1, sp, LANE), F32), V((KW, sp // NY, LANE), F32),
        DMA((steps,)), DMA((steps,)), DMA(()), DMA((NY,)), DMA((NY - 1,)),
        DMA((nz - 1,)), DMA((nz - 1,)), DMA((nc - 1,)), DMA((nc - 1,)), DMA((nc - 1,)), DMA((nc - 1,)),
        DMA((NY - 1, nc)), DMA((NY - 1, nc)),
        DMA((2, (NY - 1) * PARTS)), DMA((2, (NY - 1) * PARTS)), DMA((NY - 1,)), DMA((NY - 1,)),
        DMA((nc - 1,)), DMA((nc,)),
    ]
    hbm = pl.BlockSpec(memory_space=pl.ANY)

    def body(*refs):
        kernel((nz, nc, nl, nb, ns), *refs)

    got = pl.pallas_call(
        body,
        out_shape=jax.ShapeDtypeStruct((KW, sp // NY, LANE), F32),
        in_specs=[hbm, hbm, hbm],
        out_specs=pl.BlockSpec(memory_space=pltpu.VMEM),
        scratch_shapes=scratch,
        compiler_params=pltpu.CompilerParams(
            collective_id=0, has_side_effects=True, vmem_limit_bytes=56 * 2 ** 20
        ),
        name="solve_window",
    )(
        factor.reshape(nl * nb * KW, lanes),
        knowns.reshape(nl * nb, ns),
        inverse,
    )
    return -jnp.transpose(got, (0, 2, 1))


def solution(mesh):
    nz, nc = mesh.shape["row"] // NY, mesh.shape["col"]

    def step(factor, knowns, inverse):
        return on_device(nz, nc, factor, knowns, inverse)

    return jax.shard_map(
        step,
        mesh=mesh,
        in_specs=(
            P("row", None, None, None, "col"),
            P("row", None, None, None),
            P(None, None, "col"),
        ),
        out_specs=P(None, "col", "row"),
        check_vma=False,
    )
```

```python
import jax
import jax.numpy as jnp
from jax import lax
from jax.experimental import pallas as pl
from jax.experimental.pallas import tpu as pltpu
from jax.sharding import PartitionSpec as P

MESH = pl.DeviceIdType.MESH
KW = 4
NY = 4
LANE = 128
STEP = 512
TILE = 256
PARTS = 8
F32 = jnp.float32
BF16 = jnp.bfloat16
POINTS = (6, 15, 26, 33)
HOP = 4


def halves(value):
    high = value.astype(BF16)
    low = (value - high.astype(F32)).astype(BF16)
    return high, low


def mul(a, b):
    return jnp.dot(a, b, preferred_element_type=F32)


def kernel(
    sizes,
    fac, kn, inv, out,
    fbuf, kbuf, dfull, kth, ktl, acc, ybuf, zsrc, zbuf, tfull, racc, cbuf, lhs,
    dh, dl, ubuf, uh, ul, wh, wl, xfull, csrc, obuf,
    fsem, ksem, dsem, ysend, yrecv, zsend, zrecv, tsend, trecv, xsend, xrecv,
    csend, crecv, usend, urecv, osend, orecv, dsend, drecv,
):
    nz, nc, nl, nb, ns = sizes
    sp = ns // nz
    so = sp // NY
    per = nb // STEP
    row, col = lax.axis_index("row"), lax.axis_index("col")
    z, y = lax.div(row, NY), lax.rem(row, NY)
    last = nz - 1
    nblk = NY - 1 - y
    nf = nblk * PARTS
    crows = nb // (2 * PARTS)

    def remote(src, dst, ssem, rsem, to_row, to_col):
        return pltpu.make_async_remote_copy(
            src_ref=src, dst_ref=dst, send_sem=ssem, recv_sem=rsem,
            device_id=(to_row, to_col), device_id_type=MESH,
        )

    def load_f(c):
        rows = pl.ds(c * STEP * KW, STEP * KW)
        return pltpu.make_async_copy(fac.at[rows], fbuf.at[rows], fsem.at[c])

    def load_k(c):
        rows = pl.ds(c * STEP, STEP)
        return pltpu.make_async_copy(kn.at[rows], kbuf.at[rows], ksem.at[c])

    def load_d():
        return pltpu.make_async_copy(inv.at[y], dfull.at[col], dsem)

    steps = nl * per
    own = (nl - 1) * per

    @pl.when(z == last)
    def _():
        for c in range(own, steps):
            load_f(c).start()

    barrier = pltpu.get_barrier_semaphore()
    for dy in range(NY):
        for dk in range(nc):
            if dy or dk:
                pl.semaphore_signal(
                    barrier, inc=1,
                    device_id=(z * NY + lax.rem(y + dy, NY), lax.rem(col + dk, nc)),
                    device_id_type=MESH,
                )
    for d in range(1, nz):
        pl.semaphore_signal(
            barrier, inc=1, device_id=(lax.rem(z + d, nz) * NY + y, col), device_id_type=MESH
        )

    load_d().start()

    for c in range(own):
        load_f(c).start()
        load_k(c).start()

    @pl.when(z < last)
    def _():
        for c in range(own, steps):
            load_f(c).start()

    for c in range(own, steps):
        load_k(c).start()

    def enter():
        pl.semaphore_wait(barrier, NY * nc - 1 + nz - 1)

    def piece(way, f):
        first = way * (nb // 2) + lax.rem(f, PARTS) * crows
        return ubuf.at[lax.div(f, PARTS), pl.ds(pl.multiple_of(first, 8), crows)]

    def pass_on(way, f):
        to = lax.rem(z + (1 if way == 0 else nz - 1), nz)
        part = piece(way, f)
        return remote(part, part, usend.at[way, f], urecv.at[way, f], to * NY + y, col)

    def feed():
        for c in range(own, steps):
            load_f(c).wait()

        @pl.loop(0, nf)
        def _(f):
            j = y + 1 + lax.div(f, PARTS)
            for way in (0, 1):
                first = way * (nb // 2) + lax.rem(f, PARTS) * crows
                start = (nl - 1) * nb * KW + first * KW + j
                ubuf[lax.div(f, PARTS), pl.ds(pl.multiple_of(first, 8), crows), :] = fbuf[
                    pl.ds(start, crows, stride=KW), :
                ]
                pass_on(way, f).start()

    core = lax.rem(col, 2)
    partner = col + 1 - 2 * core
    middle = jnp.logical_and(y > 0, y < NY - 1)

    def d_slot(d):
        return lax.rem(col + 2 * d, nc)

    def d_out(d):
        mine = dfull.at[col]
        return remote(mine, mine, dsend.at[d], drecv.at[col], row, d_slot(d) if d else partner)

    def d_relay(d):
        part = dfull.at[d_slot(d)]
        return remote(part, part, dsend.at[nc // 2 - 1 + d], drecv.at[d_slot(d)], row, partner)

    def d_in(slot):
        part = dfull.at[slot]
        return remote(part, part, dsend.at[0], drecv.at[slot], row, partner)

    def share_d():
        load_d().wait()

        @pl.when(middle)
        def _():
            for d in range(nc // 2):
                d_out(d).start()

    def take_d():
        for d in range(1, nc // 2):
            d_in(d_slot(d)).wait_recv()
            d_relay(d).start()
        for d in range(nc // 2):
            d_in(lax.rem(partner + 2 * d, nc)).wait_recv()

    def fold(count):
        high, low = uh[count], ul[count]

        @pl.loop(0, nb // TILE)
        def _(c):
            rows = pl.ds(pl.multiple_of(c * TILE, TILE), TILE)
            a, l = halves(jnp.concatenate([dfull[k, rows, :] for k in range(nc)], axis=1))
            got = mul(a, high) + mul(l, high) + mul(a, low)
            wh[count, rows, :], wl[count, rows, :] = halves(got)

    def at_end(way):
        return (z == last - 1) if way == 0 else (z == 0)

    def relay(since, until):
        @pl.when(z < last)
        def _():
            @pl.loop(since, until)
            def _(t):
                for way in (0, 1):
                    hop = z + 1 if way == 0 else last - z
                    f = t - HOP * hop

                    @pl.when(jnp.logical_and(f >= 0, f < nf))
                    def _():
                        pass_on(way, f).wait_recv()

                        @pl.when(jnp.logical_not(at_end(way)))
                        def _():
                            pass_on(way, f).start()

    def multiply(c, half, first):
        rows = pl.ds(pl.multiple_of(c * STEP, STEP), STEP)
        if half == 0:
            load_f(c).wait()
            load_k(c).wait()
            high, low = halves(kbuf[rows, :].T)
            kth[c] = high
            ktl[c] = low
        else:
            high, low = kth[c], ktl[c]
        fh, fl = [], []
        for j in (2 * half, 2 * half + 1):
            a, b = halves(fbuf[pl.ds(c * STEP * KW + j, STEP, stride=KW), :])
            fh.append(a)
            fl.append(b)
        fh, fl = jnp.concatenate(fh, axis=1), jnp.concatenate(fl, axis=1)
        got = mul(high, fh) + mul(low, fh) + mul(high, fl)
        for n in (0, 1):
            part = got[:, n * LANE:(n + 1) * LANE]
            if first:
                acc[2 * half + n] = part
            else:
                acc[2 * half + n] += part

    def to_row(j):
        slot = lax.rem(y - j + NY, NY) - 1
        return remote(acc.at[j], ybuf.at[slot], ysend.at[j], yrecv.at[slot], z * NY + j, col)

    for half in (0, 1):
        if half == 0:
            @pl.when(z == last)
            def _():
                enter()
                feed()

        multiply(0, half, True)
        if half == 0:
            @pl.when(z < last)
            def _():
                enter()

            share_d()

        @pl.loop(1, own)
        def _(c):
            multiply(c, half, False)
            if half == 1:
                relay(POINTS[0] + c - 1, POINTS[0] + c)

        @pl.when(z < last)
        def _():
            @pl.loop(own, steps)
            def _(c):
                multiply(c, half, False)
                if half == 1:
                    relay(POINTS[0] + c - 1, POINTS[0] + c)

        for j in (2 * half, 2 * half + 1):
            @pl.when(y != j)
            def _():
                to_row(j).start()

        relay(0 if half == 0 else POINTS[0] + steps - 1, POINTS[half])

    for c in range(per):
        rows = pl.ds(c * STEP, STEP)
        a, b = halves(dfull[col, rows, :])
        dh[rows, :] = a
        dl[rows, :] = b

    @pl.when(z == last)
    def _():
        for c in range(own, steps):
            load_k(c).wait()
        first = pl.multiple_of((nl - 1) * nb + col * LANE, LANE)
        acc[y] -= kbuf[pl.ds(first, LANE), :].T

    for slot in range(NY - 1):
        remote(acc.at[0], ybuf.at[slot], ysend.at[0], yrecv.at[slot], row, col).wait_recv()
    zsrc[...] = acc[y] + ybuf[0] + ybuf[1] + ybuf[2]

    def to_plane(d):
        to = lax.rem(z + d, nz)
        return remote(
            zsrc.at[pl.ds(pl.multiple_of(to * sp, 8), sp)], zbuf.at[d - 1],
            zsend.at[d - 1], zrecv.at[d - 1], to * NY + y, col,
        )

    for d in range(1, nz):
        to_plane(d).start()
    relay(POINTS[1], POINTS[2])
    total = zsrc[pl.ds(pl.multiple_of(z * sp, 8), sp), :]
    for d in range(1, nz):
        to_plane(d).wait_recv()
        total += zbuf[d - 1]
    tfull[col] = total

    def to_cols(full, ssem, rsem, d):
        return remote(full.at[col], full.at[col], ssem.at[d - 1], rsem.at[d - 1], row, lax.rem(col + d, nc))

    def from_cols(full, ssem, rsem, d):
        slot = lax.rem(col - d + nc, nc)
        return remote(full.at[slot], full.at[slot], ssem.at[d - 1], rsem.at[d - 1], row, col)

    for d in range(1, nc):
        to_cols(tfull, tsend, trecv, d).start()
    relay(POINTS[2], POINTS[3])
    for d in range(1, nc):
        from_cols(tfull, tsend, trecv, d).wait_recv()
    racc[...] = tfull[...]

    def split_u(b):
        for c in range(per):
            rows = pl.ds(c * STEP, STEP)
            a, l = halves(ubuf[b, rows, :])
            uh[b, rows, :] = a
            ul[b, rows, :] = l

    def finish(b):
        so_far = POINTS[3] if b == 0 else max(POINTS[3], PARTS * b + HOP * (nz - 1))
        relay(so_far, PARTS * (b + 1) + HOP * (nz - 1))
        split_u(b)

    @pl.when(middle)
    def _():
        finish(0)
        take_d()
        fold(0)

    for b in range(1, NY - 2):
        @pl.when(jnp.logical_and(y > 0, b < nblk))
        def _():
            finish(b)

    @pl.loop(0, y)
    def _(i):
        for k in range(nc):
            remote(csrc.at[0], cbuf.at[i, k], csend.at[0, k], crecv.at[i, k], row, col).wait_recv()
        racc[...] -= cbuf[i]

    def fill(full):
        for k in range(nc):
            a, b = halves(full[k])
            lhs[0:sp, k * LANE:(k + 1) * LANE] = a
            lhs[sp:2 * sp, k * LANE:(k + 1) * LANE] = b

    def apply(high, low):
        both = mul(lhs[...], high)
        return both[0:sp] + both[sp:2 * sp] + mul(lhs[0:sp, :], low)

    def to_later(b, k):
        return remote(
            csrc.at[b], cbuf.at[y, col], csend.at[b, k], crecv.at[y, col], z * NY + y + 1 + b, k
        )

    def correct(b, high, low):
        csrc[b] = apply(high[b], low[b])
        for k in range(nc):
            to_later(b, k).start()

    fill(racc)
    for count in range(1, NY - 1):
        @pl.when(y == NY - 1 - count)
        def _():
            for b in range(count):
                if b:
                    fold(b)
                correct(b, wh, wl)

    xfull[col] = apply(dh[...], dl[...])

    @pl.when(y == 0)
    def _():
        for d in range(1, nc):
            to_cols(xfull, xsend, xrecv, d).start()

    def to_owner(d):
        to = lax.rem(y + d, NY)
        return remote(
            xfull.at[col, pl.ds(pl.multiple_of(to * so, 8), so)], obuf.at[y],
            osend.at[d - 1], orecv.at[d - 1], z * NY + to, col,
        )

    for d in range(1, NY):
        to_owner(d).start()
    obuf[y] = xfull[col, pl.ds(pl.multiple_of(y * so, 8), so), :]

    @pl.when(y == 0)
    def _():
        finish(0)
        for d in range(1, nc):
            from_cols(xfull, xsend, xrecv, d).wait_recv()
        fill(xfull)
        for b in range(NY - 1):
            if b > 0:
                finish(b)
            correct(b, uh, ul)

    for d in range(1, NY):
        slot = lax.rem(y - d + NY, NY)
        remote(obuf.at[slot], obuf.at[slot], osend.at[d - 1], orecv.at[d - 1], row, col).wait_recv()
    out[...] = obuf[...]

    for j in range(NY):
        @pl.when(y != j)
        def _():
            to_row(j).wait_send()
    for d in range(1, nz):
        to_plane(d).wait_send()
    for d in range(1, nc):
        to_cols(tfull, tsend, trecv, d).wait_send()

    @pl.when(y == 0)
    def _():
        for d in range(1, nc):
            to_cols(xfull, xsend, xrecv, d).wait_send()

    @pl.loop(0, nblk)
    def _(b):
        for k in range(nc):
            to_later(b, k).wait_send()

    @pl.when(middle)
    def _():
        for d in range(nc // 2):
            d_out(d).wait_send()
        for d in range(1, nc // 2):
            d_relay(d).wait_send()

    for d in range(1, NY):
        to_owner(d).wait_send()

    @pl.loop(0, nf)
    def _(f):
        for way in (0, 1):
            @pl.when(jnp.logical_not(at_end(way)))
            def _():
                pass_on(way, f).wait_send()


def on_device(nz, nc, factor, knowns, inverse):
    _, nl, nb, _, lanes = factor.shape
    ns = knowns.shape[3]
    sp = ns // nz
    steps = nl * (nb // STEP)
    V, DMA = pltpu.VMEM, pltpu.SemaphoreType.DMA
    scratch = [
        V((nl * nb * KW, LANE), F32), V((nl * nb, ns), F32), V((nc, nb, LANE), F32),
        V((steps, ns, STEP), BF16), V((steps, ns, STEP), BF16),
        V((KW, ns, LANE), F32), V((NY - 1, ns, LANE), F32),
        V((ns, LANE), F32), V((nz - 1, sp, LANE), F32),
        V((nc, sp, LANE), F32), V((nc, sp, LANE), F32),
        V((NY - 1, nc, sp, LANE), F32), V((2 * sp, nb), BF16),
        V((nb, LANE), BF16), V((nb, LANE), BF16),
        V((NY - 1, nb, LANE), F32), V((NY - 1, nb, LANE), BF16), V((NY - 1, nb, LANE), BF16),
        V((NY - 2, nb, LANE), BF16), V((NY - 2, nb, LANE), BF16),
        V((nc, sp, LANE), F32), V((NY - 1, sp, LANE), F32), V((KW, sp // NY, LANE), F32),
        DMA((steps,)), DMA((steps,)), DMA(()), DMA((NY,)), DMA((NY - 1,)),
        DMA((nz - 1,)), DMA((nz - 1,)), DMA((nc - 1,)), DMA((nc - 1,)), DMA((nc - 1,)), DMA((nc - 1,)),
        DMA((NY - 1, nc)), DMA((NY - 1, nc)),
        DMA((2, (NY - 1) * PARTS)), DMA((2, (NY - 1) * PARTS)), DMA((NY - 1,)), DMA((NY - 1,)),
        DMA((nc - 1,)), DMA((nc,)),
    ]
    hbm = pl.BlockSpec(memory_space=pl.ANY)

    def body(*refs):
        kernel((nz, nc, nl, nb, ns), *refs)

    got = pl.pallas_call(
        body,
        out_shape=jax.ShapeDtypeStruct((KW, sp // NY, LANE), F32),
        in_specs=[hbm, hbm, hbm],
        out_specs=pl.BlockSpec(memory_space=pltpu.VMEM),
        scratch_shapes=scratch,
        compiler_params=pltpu.CompilerParams(
            collective_id=0, has_side_effects=True, vmem_limit_bytes=56 * 2 ** 20
        ),
        name="solve_window",
    )(
        factor.reshape(nl * nb * KW, lanes),
        knowns.reshape(nl * nb, ns),
        inverse,
    )
    return -jnp.transpose(got, (0, 2, 1))


def solution(mesh):
    nz, nc = mesh.shape["row"] // NY, mesh.shape["col"]

    def step(factor, knowns, inverse):
        return on_device(nz, nc, factor, knowns, inverse)

    return jax.shard_map(
        step,
        mesh=mesh,
        in_specs=(
            P("row", None, None, None, "col"),
            P("row", None, None, None),
            P(None, None, "col"),
        ),
        out_specs=P(None, "col", "row"),
        check_vma=False,
    )
```
